256 devices in a mesh: seq: 64 (over x_hi, y, z), kvh: 4 (over x_lo, core).
Axes of the slice: x: 4 (x_hi: 2, x_lo: 2; x = x_hi * 2 + x_lo), y: 4, z: 8, core: 2. Of those that a mesh axis runs over, the one named last changes fastest.
Arguments:
- queries: bfloat16 [32768, 4096], P(('seq', 'kvh')), may hold values from -5 to 5
- key_rows: bfloat16 [32768, 2048], P(('seq', 'kvh')), may hold values from -6 to 6
- value_rows: bfloat16 [32768, 2048], P(('seq', 'kvh')), may hold values from -6 to 6
- grad_out: bfloat16 [32768, 4096], P(('seq', 'kvh')), may hold values from -6 to 6
Outputs:
- attended: bfloat16 [32768, 4096], P(('seq', 'kvh'))
- grad_queries: bfloat16 [32768, 4096], P(('seq', 'kvh'))
- grad_keys: bfloat16 [32768, 2048], P(('seq', 'kvh'))
- grad_values: bfloat16 [32768, 2048], P(('seq', 'kvh'))
The draws below stay inside these ranges and needn't reach their ends.
All inputs are finite; a program needn't handle non-finite values.
Results may differ from the reference program's by a relative error of at most 0.012.
Values may be sent and summed in bfloat16 or wider, within the bound.
A program may use at most 128 MiB of HBM per device.

```python
import jax
import jax.numpy as jnp
from jax import lax

QHEADS = 32
KVHEADS = 16
HEAD_DIM = 128
WINDOW = 1024
TOKENS = 32768


def draw_queries(key, part):
    base = jax.random.normal(jax.random.fold_in(key, 1), (TOKENS, KVHEADS, 2, HEAD_DIM), jnp.float32)
    base = jnp.clip(base, -5.0, 5.0)
    return base.reshape(TOKENS, QHEADS * HEAD_DIM).astype(jnp.bfloat16)


def draw_key_rows(key, part):
    base = jax.random.normal(jax.random.fold_in(key, 2), (TOKENS, KVHEADS, HEAD_DIM), jnp.float32)
    base = jnp.clip(base, -5.0, 5.0)
    return base.reshape(TOKENS, KVHEADS * HEAD_DIM).astype(jnp.bfloat16)


def level_of(rng, extent, split, smallest, top_value):
    level, own = 1.0, jax.random.fold_in(rng, 6)
    for axis_at, blocks in split:
        heights = jnp.exp(jax.random.uniform(jax.random.fold_in(own, axis_at), (blocks,), jnp.float32, smallest / len(split), top_value / len(split)))
        level = level * jnp.repeat(heights, extent[axis_at] // blocks).reshape([-1 if axis == axis_at else 1 for axis in range(len(extent))])
    return level


def gaussian(own_key, dims, scale, limit, split=(), kind=jnp.bfloat16):
    array = jax.random.normal(own_key, dims, jnp.float32) * scale
    if len(split) > 0:
        array = level_of(own_key, dims, split, -0.22, 0.18) * array
    return jnp.clip(array, min=-limit, max=limit).astype(kind)


def setup_inputs(seed: int = 0) -> dict:
    seeds = jax.random.split(jax.random.key(seed), 5)
    queries = draw_queries(jax.random.fold_in(seeds[4], 71), 0)
    key_rows = draw_key_rows(jax.random.fold_in(seeds[4], 71), 0)
    value_rows = gaussian(seeds[2], (TOKENS, KVHEADS * HEAD_DIM), 1.0, 6.0, ((0, 256),))
    grad_out = gaussian(seeds[3], (TOKENS, QHEADS * HEAD_DIM), 1.0, 6.0, ((0, 256),))
    return {"queries": queries, "key_rows": key_rows, "value_rows": value_rows, "grad_out": grad_out}


score_scale = 168.0 ** -0.5


def reference(queries, key_rows, value_rows, grad_out):
    block = WINDOW // 2
    span = WINDOW + block
    blocks = TOKENS // block
    kv_count = key_rows.shape[1] // HEAD_DIM
    width_kv = key_rows.shape[1]
    padding = jnp.zeros((WINDOW, width_kv), key_rows.dtype)
    keys_pad = jnp.concatenate([padding, key_rows], axis=0)
    values_pad = jnp.concatenate([padding, value_rows], axis=0)
    highest = lax.Precision.HIGHEST

    def one_block(totals, number):
        grad_k_acc, grad_v_acc = totals
        start_row = (number * block).astype(jnp.int32)
        q_blk = lax.dynamic_slice_in_dim(queries, start_row, block, 0).astype(jnp.float32).reshape(block, kv_count, 2, HEAD_DIM)
        o_blk = lax.dynamic_slice_in_dim(grad_out, start_row, block, 0).astype(jnp.float32).reshape(block, kv_count, 2, HEAD_DIM)
        k_blk = lax.dynamic_slice_in_dim(keys_pad, start_row, span, 0).astype(jnp.float32).reshape(span, kv_count, HEAD_DIM)
        v_blk = lax.dynamic_slice_in_dim(values_pad, start_row, span, 0).astype(jnp.float32).reshape(span, kv_count, HEAD_DIM)
        query_pos = start_row + jnp.arange(block, dtype=jnp.int32)
        key_pos = start_row - WINDOW + jnp.arange(span, dtype=jnp.int32)
        allowed = (key_pos[None, :] <= query_pos[:, None]) & (query_pos[:, None] - key_pos[None, :] < WINDOW) & (key_pos[None, :] >= 0)
        scores = jnp.einsum("rgjd,kgd->gjrk", q_blk, k_blk, precision=highest) * score_scale
        scores = jnp.where(allowed[None, None], scores, -jnp.inf)
        row_max = jnp.max(scores, axis=-1, keepdims=True)
        exponent = jnp.exp(scores - row_max)
        weights = exponent / jnp.sum(exponent, axis=-1, keepdims=True)
        weights_low = lax.optimization_barrier(weights.astype(jnp.bfloat16)).astype(jnp.float32)
        out_blk = jnp.einsum("gjrk,kgd->rgjd", weights_low, v_blk, precision=highest)
        grad_weights = jnp.einsum("rgjd,kgd->gjrk", o_blk, v_blk, precision=highest)
        row_delta = jnp.sum(weights * grad_weights, axis=-1, keepdims=True)
        grad_scores = lax.optimization_barrier((weights * (grad_weights - row_delta)).astype(jnp.bfloat16)).astype(jnp.float32)
        dq_blk = jnp.einsum("gjrk,kgd->rgjd", grad_scores, k_blk, precision=highest) * score_scale
        dk_part = jnp.einsum("gjrk,rgjd->kgd", grad_scores, q_blk, precision=highest) * score_scale
        dv_part = jnp.einsum("gjrk,rgjd->kgd", weights_low, o_blk, precision=highest)
        old_k = lax.dynamic_slice_in_dim(grad_k_acc, start_row, span, 0)
        old_v = lax.dynamic_slice_in_dim(grad_v_acc, start_row, span, 0)
        grad_k_acc = lax.dynamic_update_slice_in_dim(grad_k_acc, old_k + dk_part.reshape(span, width_kv), start_row, 0)
        grad_v_acc = lax.dynamic_update_slice_in_dim(grad_v_acc, old_v + dv_part.reshape(span, width_kv), start_row, 0)
        outputs = (out_blk.reshape(block, -1).astype(jnp.bfloat16), dq_blk.reshape(block, -1).astype(jnp.bfloat16))
        return (grad_k_acc, grad_v_acc), outputs

    initial = (jnp.zeros((TOKENS + WINDOW, width_kv), jnp.float32), jnp.zeros((TOKENS + WINDOW, width_kv), jnp.float32))
    totals, outputs = lax.scan(one_block, initial, jnp.arange(blocks, dtype=jnp.int32))
    attended = outputs[0].reshape(TOKENS, -1)
    grad_queries = outputs[1].reshape(TOKENS, -1)
    grad_keys = totals[0][WINDOW:].astype(jnp.bfloat16)
    grad_values = totals[1][WINDOW:].astype(jnp.bfloat16)
    return (attended, grad_queries, grad_keys, grad_values)
```

```python
import math

import jax
import jax.numpy as jnp
from jax import lax
from jax.experimental import pallas as pl
from jax.experimental.pallas import tpu as pltpu
from jax.sharding import PartitionSpec as P


HEAD_DIM = 128
WINDOW = 1024
MESH = pl.DeviceIdType.MESH
NEG = -1e30
BIG = 1e30
SCALE = 168.0 ** (-0.5)
SCALE2 = SCALE * math.log2(math.e)
F32 = jnp.float32
BF16 = jnp.bfloat16
ROWS = 128
PEERS = 4
HEADS = 4
OWN = PEERS * ROWS
SPAN = WINDOW + OWN
KEYS = WINDOW + ROWS
BLOCKS = KEYS // ROWS


def kernel(
    n_seq,
    q_ref,
    k_ref,
    v_ref,
    g_ref,
    o_out,
    dq_out,
    dk_out,
    dv_out,
    kv,
    qd,
    od,
    grad,
    first_stage,
    second_stage,
    last_stage,
    got_first,
    got_second,
    k_t,
    v_t,
    scores,
    probs,
    dscores,
    kv_in,
    qd_in,
    in_send,
    halo_recv,
    halo_send,
    grad_recv,
    grad_send,
    out_recv,
    out_send,
):
    seq = lax.axis_index("seq")
    kvh = lax.axis_index("kvh")
    half = n_seq // 2

    def slot_of(group, position):
        return lax.rem(position + 2 * lax.div(group, half), PEERS)

    slot = slot_of(seq, kvh)
    has_prev = seq > 0
    has_next = seq < n_seq - 1
    prev = (seq - 1, slot_of(seq - 1, slot))
    next_ = (seq + 1, slot_of(seq + 1, slot))

    def await_bytes(ref, sem):
        pltpu.make_async_copy(ref, ref, sem).wait()

    barrier = pltpu.get_barrier_semaphore()
    for step in range(1, PEERS):
        pl.semaphore_signal(
            barrier, inc=1, device_id=(seq, lax.rem(kvh + step, PEERS)), device_id_type=MESH
        )

    @pl.when(has_prev)
    def _():
        pl.semaphore_signal(barrier, inc=1, device_id=prev, device_id_type=MESH)

    @pl.when(has_next)
    def _():
        pl.semaphore_signal(barrier, inc=1, device_id=next_, device_id_type=MESH)

    neighbours = has_prev.astype(jnp.int32) + has_next.astype(jnp.int32)
    pl.semaphore_wait(barrier, PEERS - 1 + neighbours)

    my_rows = pl.ds(pl.multiple_of(WINDOW + kvh * ROWS, ROWS), ROWS)
    my_own = pl.ds(pl.multiple_of(kvh * ROWS, ROWS), ROWS)

    def send_inputs(head, carry):
        for array, (source, wide, buffer) in enumerate(
            ((k_ref, 1, kv), (v_ref, 1, kv), (q_ref, 2, qd), (g_ref, 2, qd))
        ):
            width = wide * HEAD_DIM
            for step in range(PEERS):
                position = lax.rem(kvh + step, PEERS)
                column = (slot_of(seq, position) * HEADS + head) * width
                src = source.at[:, pl.ds(pl.multiple_of(column, HEAD_DIM), width)]
                dst = buffer.at[head, array % 2, my_rows if wide == 1 else my_own, :]
                sem = kv_in.at[head] if wide == 1 else qd_in.at[head]
                if step == 0:
                    pltpu.make_async_copy(src, dst, sem).start()
                else:
                    pltpu.make_async_remote_copy(
                        src_ref=src,
                        dst_ref=dst,
                        send_sem=in_send.at[array],
                        recv_sem=sem,
                        device_id=(seq, position),
                        device_id_type=MESH,
                    ).start()
        return carry

    lax.fori_loop(0, HEADS, send_inputs, 0)

    @pl.when(jnp.logical_not(has_prev))
    def _():
        for head in range(HEADS):
            kv[head, :, pl.ds(0, WINDOW), :] = jnp.zeros((2, WINDOW, HEAD_DIM), BF16)

    @pl.when(jnp.logical_not(has_next))
    def _():
        got_first[...] = jnp.zeros(got_first.shape, BF16)
        got_second[...] = jnp.zeros(got_second.shape, BF16)

    def halo(head, hop):
        return pltpu.make_async_remote_copy(
            src_ref=kv.at[head, :, pl.ds(WINDOW - hop * OWN, OWN), :],
            dst_ref=kv.at[head, :, pl.ds(WINDOW - (hop + 1) * OWN, OWN), :],
            send_sem=halo_send.at[hop, head],
            recv_sem=halo_recv.at[hop, head],
            device_id=next_,
            device_id_type=MESH,
        )

    def send_own(head):
        await_bytes(kv.at[head, :, pl.ds(WINDOW, OWN), :], kv_in.at[head])

        @pl.when(has_next)
        def _():
            halo(head, 0).start()

    def pass_on(head):
        @pl.when(has_prev)
        def _():
            await_bytes(kv.at[head, :, pl.ds(OWN, OWN), :], halo_recv.at[0, head])

        @pl.when(has_next)
        def _():
            halo(head, 1).start()

    def await_halo(head):
        @pl.when(has_prev)
        def _():
            await_bytes(kv.at[head, :, pl.ds(0, OWN), :], halo_recv.at[1, head])

    def grad_copy(stage, buffer, hop, head):
        return pltpu.make_async_remote_copy(
            src_ref=stage.at[head],
            dst_ref=buffer.at[head],
            send_sem=grad_send.at[hop, head],
            recv_sem=grad_recv.at[hop, head],
            device_id=prev,
            device_id_type=MESH,
        )

    def grads_first(head):
        for half_ in range(2):
            first_stage[head, half_] = grad[head, half_, pl.ds(0, OWN), :].astype(BF16)

        @pl.when(has_prev)
        def _():
            grad_copy(first_stage, got_first, 0, head).start()

    def grads_second(head):
        @pl.when(has_next)
        def _():
            await_bytes(got_first.at[head], grad_recv.at[0, head])

        for half_ in range(2):
            second_stage[head, half_] = (
                grad[head, half_, pl.ds(OWN, OWN), :] + got_first[head, half_].astype(F32)
            ).astype(BF16)

        @pl.when(has_prev)
        def _():
            grad_copy(second_stage, got_second, 1, head).start()

    def send_back(source, wide, out, array, head):
        width = wide * HEAD_DIM
        column = pl.multiple_of((slot * HEADS + head) * width, HEAD_DIM)
        for step in range(PEERS):
            position = lax.rem(kvh + step, PEERS)
            src = source.at[pl.ds(pl.multiple_of(position * ROWS, ROWS), ROWS), :]
            dst = out.at[:, pl.ds(column, width)]
            if step == 0:
                pltpu.make_async_copy(src, dst, out_recv.at[array]).start()
            else:
                pltpu.make_async_remote_copy(
                    src_ref=src,
                    dst_ref=dst,
                    send_sem=out_send.at[array],
                    recv_sem=out_recv.at[array],
                    device_id=(seq, position),
                    device_id_type=MESH,
                ).start()

    def grads_last(head):
        @pl.when(has_next)
        def _():
            await_bytes(got_second.at[head], grad_recv.at[1, head])

        for half_ in range(2):
            last_stage[head, half_] = (
                grad[head, half_, pl.ds(WINDOW, OWN), :] + got_second[head, half_].astype(F32)
            ).astype(BF16)
        send_back(last_stage.at[head, 0], 1, dk_out, 2, head)
        send_back(last_stage.at[head, 1], 1, dv_out, 3, head)

    low = jnp.where(seq == 0, WINDOW // ROWS, jnp.where(seq == 1, (WINDOW - OWN) // ROWS, 0))
    key_at = lax.broadcasted_iota(jnp.int32, (ROWS, 2 * ROWS), 0)
    row_at = lax.rem(lax.broadcasted_iota(jnp.int32, (ROWS, 2 * ROWS), 1), ROWS)

    def turned(block):
        block = block.astype(F32)
        return jnp.concatenate(
            [block[:, :HEAD_DIM].T, block[:, HEAD_DIM:].T], axis=1
        )

    def dot(a, b):
        return jnp.dot(a, b, preferred_element_type=F32)

    def dot_t(a, b):
        return lax.dot_general(a, b, (((1,), (1,)), ((), ())), preferred_element_type=F32)

    def transposed_keys(head):
        for piece in range(SPAN // ROWS):
            rows = pl.ds(piece * ROWS, ROWS)
            k_t[:, rows] = kv[head, 0, rows, :].astype(F32).T.astype(BF16)
            v_t[:, rows] = kv[head, 1, rows, :].astype(F32).T.astype(BF16)

    def query_block(head, block):
        start = pl.multiple_of(block * ROWS, ROWS)
        rows = pl.ds(start, ROWS)
        q_t = turned(qd[head, 0, rows, :])
        g_t = turned(qd[head, 1, rows, :])
        q_low = q_t.astype(BF16)
        g_low = g_t.astype(BF16)
        top = None
        for piece in range(BLOCKS):
            keys = kv[head, 0, pl.ds(start + piece * ROWS, ROWS), :]
            s = dot(keys, q_low)
            if piece == 0:
                s = jnp.where(key_at > row_at, s, NEG)
            if piece == BLOCKS - 1:
                s = jnp.where(key_at <= row_at, s, NEG)
            scores[pl.ds(piece * ROWS, ROWS), :] = s
            best = s.reshape(ROWS // 8, 8, 2 * ROWS).max(axis=0)
            if piece < BLOCKS - 1:
                best = jnp.where(block + piece >= low, best, NEG)
            top = best if top is None else jnp.maximum(top, best)
        top = top.max(axis=0, keepdims=True) * SCALE2
        total = jnp.zeros((8, 2 * ROWS), F32)
        for piece in range(BLOCKS):
            here = pl.ds(piece * ROWS, ROWS)
            shift = top
            if piece < BLOCKS - 1:
                shift = jnp.where(block + piece >= low, top, BIG)
            p = jnp.exp2(scores[here, :] * SCALE2 - shift)
            total = total + p.reshape(ROWS // 8, 8, 2 * ROWS).sum(axis=0)
            probs[here, :] = p.astype(BF16)
        inverse = 1.0 / total.sum(axis=0, keepdims=True)
        window = pl.ds(start, KEYS)
        o_t = dot(v_t[:, window], probs[...]) * inverse
        delta = (o_t * g_t).sum(axis=0, keepdims=True)
        q_scaled = (q_t * (inverse * SCALE)).astype(BF16)
        g_scaled = (g_t * inverse).astype(BF16)
        for piece in range(BLOCKS):
            here = pl.ds(piece * ROWS, ROWS)
            there = pl.ds(start + piece * ROWS, ROWS)
            dp = dot(kv[head, 1, there, :], g_low)
            p = probs[here, :]
            ds = (p.astype(F32) * (dp - delta)).astype(BF16)
            dscores[here, :] = ds
            dv = dot_t(p, g_scaled)
            dk = dot_t(ds, q_scaled)
            if piece < BLOCKS - 1:
                grad[head, 1, there, :] += dv
                grad[head, 0, there, :] += dk
            else:
                grad[head, 1, there, :] = dv
                grad[head, 0, there, :] = dk
        dq_t = dot(k_t[:, window], dscores[...]) * (inverse * SCALE)
        for index, value in enumerate((o_t, dq_t)):
            for side in range(2):
                cols = slice(side * ROWS, (side + 1) * ROWS)
                od[head, index, rows, cols] = value[:, cols].T.astype(BF16)

    send_own(0)
    pass_on(0)
    send_own(1)

    def one_head(head, carry):
        await_bytes(qd.at[head], qd_in.at[head])
        await_halo(head)
        grad[head, :, pl.ds(0, WINDOW), :] = jnp.zeros((2, WINDOW, HEAD_DIM), F32)
        transposed_keys(head)

        def one_block(block, carry):
            query_block(head, block)

            @pl.when((block == 1) & (head < HEADS - 1))
            def _():
                pass_on(head + 1)

            @pl.when((block == 1) & (head < HEADS - 2))
            def _():
                send_own(head + 2)

            @pl.when((block == 2) & (head > 0))
            def _():
                grads_second(head - 1)

            return carry

        lax.fori_loop(0, PEERS, one_block, 0)
        grads_first(head)
        send_back(od.at[head, 0], 2, o_out, 0, head)
        send_back(od.at[head, 1], 2, dq_out, 1, head)

        @pl.when(head > 0)
        def _():
            grads_last(head - 1)

        return carry

    lax.fori_loop(0, HEADS, one_head, 0)
    grads_second(HEADS - 1)
    grads_last(HEADS - 1)

    for array, buffer in enumerate((kv, kv, qd, qd)):
        region = pl.ds(0, OWN)
        await_bytes(buffer.at[pl.ds(0, PEERS - 1), 0, region, :], in_send.at[array])
    for hop in range(2):
        for head in range(HEADS):

            @pl.when(has_next)
            def _():
                halo(head, hop).wait_send()

            @pl.when(has_prev)
            def _():
                stage, buffer = ((first_stage, got_first), (second_stage, got_second))[hop]
                grad_copy(stage, buffer, hop, head).wait_send()

    for array, (out, stage) in enumerate(
        (
            (o_out, od.at[pl.ds(0, PEERS - 1), 0]),
            (dq_out, od.at[pl.ds(0, PEERS - 1), 1]),
            (dk_out, last_stage.at[pl.ds(0, PEERS - 1), 0]),
            (dv_out, last_stage.at[pl.ds(0, PEERS - 1), 1]),
        )
    ):
        await_bytes(stage, out_send.at[array])
        await_bytes(out, out_recv.at[array])


def solution(mesh):
    n_seq = mesh.shape["seq"]

    def step(queries, key_rows, value_rows, grad_out):
        def call(*refs):
            kernel(n_seq, *refs)

        flops = 5 * 2 * 256 * KEYS * HEAD_DIM * HEADS * PEERS
        return pl.pallas_call(
            call,
            name="window_attention",
            out_shape=(
                jax.ShapeDtypeStruct(queries.shape, BF16),
                jax.ShapeDtypeStruct(queries.shape, BF16),
                jax.ShapeDtypeStruct(key_rows.shape, BF16),
                jax.ShapeDtypeStruct(key_rows.shape, BF16),
            ),
            in_specs=[pl.BlockSpec(memory_space=pl.ANY)] * 4,
            out_specs=[pl.BlockSpec(memory_space=pl.ANY)] * 4,
            scratch_shapes=[
                pltpu.VMEM((HEADS, 2, SPAN, HEAD_DIM), BF16),
                pltpu.VMEM((HEADS, 2, OWN, 2 * HEAD_DIM), BF16),
                pltpu.VMEM((HEADS, 2, OWN, 2 * HEAD_DIM), BF16),
                pltpu.VMEM((HEADS, 2, SPAN, HEAD_DIM), F32),
                pltpu.VMEM((HEADS, 2, OWN, HEAD_DIM), BF16),
                pltpu.VMEM((HEADS, 2, OWN, HEAD_DIM), BF16),
                pltpu.VMEM((HEADS, 2, OWN, HEAD_DIM), BF16),
                pltpu.VMEM((HEADS, 2, OWN, HEAD_DIM), BF16),
                pltpu.VMEM((HEADS, 2, OWN, HEAD_DIM), BF16),
                pltpu.VMEM((HEAD_DIM, SPAN), BF16),
                pltpu.VMEM((HEAD_DIM, SPAN), BF16),
                pltpu.VMEM((KEYS, 2 * ROWS), F32),
                pltpu.VMEM((KEYS, 2 * ROWS), BF16),
                pltpu.VMEM((KEYS, 2 * ROWS), BF16),
                pltpu.SemaphoreType.DMA((HEADS,)),
                pltpu.SemaphoreType.DMA((HEADS,)),
                pltpu.SemaphoreType.DMA((4,)),
                pltpu.SemaphoreType.DMA((2, HEADS)),
                pltpu.SemaphoreType.DMA((2, HEADS)),
                pltpu.SemaphoreType.DMA((2, HEADS)),
                pltpu.SemaphoreType.DMA((2, HEADS)),
                pltpu.SemaphoreType.DMA((4,)),
                pltpu.SemaphoreType.DMA((4,)),
            ],
            compiler_params=pltpu.CompilerParams(
                collective_id=0, has_side_effects=True, vmem_limit_bytes=60 * 1024 * 1024
            ),
            cost_estimate=pl.CostEstimate(
                flops=flops, bytes_accessed=12 * 1024 * 1024, transcendentals=0
            ),
        )(queries, key_rows, value_rows, grad_out)

    spec = P(("seq", "kvh"), None)
    return jax.shard_map(
        step, mesh=mesh, in_specs=(spec,) * 4, out_specs=(spec,) * 4, check_vma=False
    )
```

```python
import math

import jax
import jax.numpy as jnp
from jax import lax
from jax.experimental import pallas as pl
from jax.experimental.pallas import tpu as pltpu
from jax.sharding import PartitionSpec as P


HEAD_DIM = 128
WINDOW = 1024
MESH = pl.DeviceIdType.MESH
NEG = -1e30
BIG = 1e30
SCALE = 168.0 ** (-0.5)
SCALE2 = SCALE * math.log2(math.e)
F32 = jnp.float32
BF16 = jnp.bfloat16
ROWS = 128
PEERS = 4
HEADS = 4
OWN = PEERS * ROWS
SPAN = WINDOW + OWN
KEYS = WINDOW + ROWS
BLOCKS = KEYS // ROWS


def kernel(
    n_seq,
    q_ref,
    k_ref,
    v_ref,
    g_ref,
    o_out,
    dq_out,
    dk_out,
    dv_out,
    kv,
    qd,
    od,
    grad,
    first_stage,
    second_stage,
    last_stage,
    got_first,
    got_second,
    k_t,
    v_t,
    scores,
    probs,
    dscores,
    kv_in,
    qd_in,
    in_send,
    halo_recv,
    halo_send,
    grad_recv,
    grad_send,
    out_recv,
    out_send,
):
    seq = lax.axis_index("seq")
    kvh = lax.axis_index("kvh")
    half = n_seq // 2

    def slot_of(group, position):
        return lax.rem(position + 2 * lax.div(group, half), PEERS)

    slot = slot_of(seq, kvh)
    has_prev = seq > 0
    has_next = seq < n_seq - 1
    prev = (seq - 1, slot_of(seq - 1, slot))
    next_ = (seq + 1, slot_of(seq + 1, slot))

    def await_bytes(ref, sem):
        pltpu.make_async_copy(ref, ref, sem).wait()

    barrier = pltpu.get_barrier_semaphore()
    for step in range(1, PEERS):
        pl.semaphore_signal(
            barrier, inc=1, device_id=(seq, lax.rem(kvh + step, PEERS)), device_id_type=MESH
        )

    @pl.when(has_prev)
    def _():
        pl.semaphore_signal(barrier, inc=1, device_id=prev, device_id_type=MESH)

    @pl.when(has_next)
    def _():
        pl.semaphore_signal(barrier, inc=1, device_id=next_, device_id_type=MESH)

    neighbours = has_prev.astype(jnp.int32) + has_next.astype(jnp.int32)
    pl.semaphore_wait(barrier, PEERS - 1 + neighbours)

    my_rows = pl.ds(pl.multiple_of(WINDOW + kvh * ROWS, ROWS), ROWS)
    my_own = pl.ds(pl.multiple_of(kvh * ROWS, ROWS), ROWS)

    def send_inputs(head, carry):
        for array, (source, wide, buffer) in enumerate(
            ((k_ref, 1, kv), (v_ref, 1, kv), (q_ref, 2, qd), (g_ref, 2, qd))
        ):
            width = wide * HEAD_DIM
            for step in range(PEERS):
                position = lax.rem(kvh + step, PEERS)
                column = (slot_of(seq, position) * HEADS + head) * width
                src = source.at[:, pl.ds(pl.multiple_of(column, HEAD_DIM), width)]
                dst = buffer.at[head, array % 2, my_rows if wide == 1 else my_own, :]
                sem = kv_in.at[head] if wide == 1 else qd_in.at[head]
                if step == 0:
                    pltpu.make_async_copy(src, dst, sem).start()
                else:
                    pltpu.make_async_remote_copy(
                        src_ref=src,
                        dst_ref=dst,
                        send_sem=in_send.at[array],
                        recv_sem=sem,
                        device_id=(seq, position),
                        device_id_type=MESH,
                    ).start()
        return carry

    lax.fori_loop(0, HEADS, send_inputs, 0)

    @pl.when(jnp.logical_not(has_prev))
    def _():
        for head in range(HEADS):
            kv[head, :, pl.ds(0, WINDOW), :] = jnp.zeros((2, WINDOW, HEAD_DIM), BF16)

    @pl.when(jnp.logical_not(has_next))
    def _():
        got_first[...] = jnp.zeros(got_first.shape, BF16)
        got_second[...] = jnp.zeros(got_second.shape, BF16)

    def halo(head, hop):
        return pltpu.make_async_remote_copy(
            src_ref=kv.at[head, :, pl.ds(WINDOW - hop * OWN, OWN), :],
            dst_ref=kv.at[head, :, pl.ds(WINDOW - (hop + 1) * OWN, OWN), :],
            send_sem=halo_send.at[hop, head],
            recv_sem=halo_recv.at[hop, head],
            device_id=next_,
            device_id_type=MESH,
        )

    def send_own(head):
        await_bytes(kv.at[head, :, pl.ds(WINDOW, OWN), :], kv_in.at[head])

        @pl.when(has_next)
        def _():
            halo(head, 0).start()

    def pass_on(head):
        @pl.when(has_prev)
        def _():
            await_bytes(kv.at[head, :, pl.ds(OWN, OWN), :], halo_recv.at[0, head])

        @pl.when(has_next)
        def _():
            halo(head, 1).start()

    def await_halo(head):
        @pl.when(has_prev)
        def _():
            await_bytes(kv.at[head, :, pl.ds(0, OWN), :], halo_recv.at[1, head])

    def grad_copy(stage, buffer, hop, head):
        return pltpu.make_async_remote_copy(
            src_ref=stage.at[head],
            dst_ref=buffer.at[head],
            send_sem=grad_send.at[hop, head],
            recv_sem=grad_recv.at[hop, head],
            device_id=prev,
            device_id_type=MESH,
        )

    def grads_first(head, block):
        rows = pl.ds(pl.multiple_of(block * ROWS, ROWS), ROWS)
        for half_ in range(2):
            first_stage[head, half_, rows, :] = grad[head, half_, rows, :].astype(BF16)

        @pl.when(has_prev)
        def _():
            pltpu.make_async_remote_copy(
                src_ref=first_stage.at[head, :, rows, :],
                dst_ref=got_first.at[head, :, rows, :],
                send_sem=grad_send.at[0, head],
                recv_sem=grad_recv.at[0, head],
                device_id=prev,
                device_id_type=MESH,
            ).start()

    def grads_second(head):
        @pl.when(has_next)
        def _():
            await_bytes(got_first.at[head], grad_recv.at[0, head])

        for half_ in range(2):
            second_stage[head, half_] = (
                grad[head, half_, pl.ds(OWN, OWN), :] + got_first[head, half_].astype(F32)
            ).astype(BF16)

        @pl.when(has_prev)
        def _():
            grad_copy(second_stage, got_second, 1, head).start()

    def send_back(source, wide, out, array, head):
        width = wide * HEAD_DIM
        column = pl.multiple_of((slot * HEADS + head) * width, HEAD_DIM)
        for step in range(PEERS):
            position = lax.rem(kvh + step, PEERS)
            src = source.at[pl.ds(pl.multiple_of(position * ROWS, ROWS), ROWS), :]
            dst = out.at[:, pl.ds(column, width)]
            if step == 0:
                pltpu.make_async_copy(src, dst, out_recv.at[array]).start()
            else:
                pltpu.make_async_remote_copy(
                    src_ref=src,
                    dst_ref=dst,
                    send_sem=out_send.at[array],
                    recv_sem=out_recv.at[array],
                    device_id=(seq, position),
                    device_id_type=MESH,
                ).start()

    def grads_last(head):
        @pl.when(has_next)
        def _():
            await_bytes(got_second.at[head], grad_recv.at[1, head])

        for half_ in range(2):
            last_stage[head, half_] = (
                grad[head, half_, pl.ds(WINDOW, OWN), :] + got_second[head, half_].astype(F32)
            ).astype(BF16)
        send_back(last_stage.at[head, 0], 1, dk_out, 2, head)
        send_back(last_stage.at[head, 1], 1, dv_out, 3, head)

    low = jnp.where(seq == 0, WINDOW // ROWS, jnp.where(seq == 1, (WINDOW - OWN) // ROWS, 0))
    key_at = lax.broadcasted_iota(jnp.int32, (ROWS, 2 * ROWS), 0)
    row_at = lax.rem(lax.broadcasted_iota(jnp.int32, (ROWS, 2 * ROWS), 1), ROWS)

    def turned(block):
        block = block.astype(F32)
        return jnp.concatenate(
            [block[:, :HEAD_DIM].T, block[:, HEAD_DIM:].T], axis=1
        )

    def dot(a, b):
        return jnp.dot(a, b, preferred_element_type=F32)

    def dot_t(a, b):
        return lax.dot_general(a, b, (((1,), (1,)), ((), ())), preferred_element_type=F32)

    def transposed_keys(head):
        for piece in range(SPAN // ROWS):
            rows = pl.ds(piece * ROWS, ROWS)
            k_t[:, rows] = kv[head, 0, rows, :].astype(F32).T.astype(BF16)
            v_t[:, rows] = kv[head, 1, rows, :].astype(F32).T.astype(BF16)

    def query_block(head, block):
        start = pl.multiple_of(block * ROWS, ROWS)
        rows = pl.ds(start, ROWS)
        q_t = turned(qd[head, 0, rows, :])
        g_t = turned(qd[head, 1, rows, :])
        q_low = q_t.astype(BF16)
        g_low = g_t.astype(BF16)
        top = None
        for piece in range(BLOCKS):
            keys = kv[head, 0, pl.ds(start + piece * ROWS, ROWS), :]
            s = dot(keys, q_low)
            if piece == 0:
                s = jnp.where(key_at > row_at, s, NEG)
            if piece == BLOCKS - 1:
                s = jnp.where(key_at <= row_at, s, NEG)
            scores[pl.ds(piece * ROWS, ROWS), :] = s
            best = s.reshape(ROWS // 8, 8, 2 * ROWS).max(axis=0)
            if piece < BLOCKS - 1:
                best = jnp.where(block + piece >= low, best, NEG)
            top = best if top is None else jnp.maximum(top, best)
        top = top.max(axis=0, keepdims=True) * SCALE2
        total = jnp.zeros((8, 2 * ROWS), F32)
        for piece in range(BLOCKS):
            here = pl.ds(piece * ROWS, ROWS)
            shift = top
            if piece < BLOCKS - 1:
                shift = jnp.where(block + piece >= low, top, BIG)
            p = jnp.exp2(scores[here, :] * SCALE2 - shift)
            total = total + p.reshape(ROWS // 8, 8, 2 * ROWS).sum(axis=0)
            probs[here, :] = p.astype(BF16)
        inverse = 1.0 / total.sum(axis=0, keepdims=True)
        window = pl.ds(start, KEYS)
        o_t = dot(v_t[:, window], probs[...]) * inverse
        delta = (o_t * g_t).sum(axis=0, keepdims=True)
        q_scaled = (q_t * (inverse * SCALE)).astype(BF16)
        g_scaled = (g_t * inverse).astype(BF16)
        for piece in range(BLOCKS):
            here = pl.ds(piece * ROWS, ROWS)
            there = pl.ds(start + piece * ROWS, ROWS)
            dp = dot(kv[head, 1, there, :], g_low)
            p = probs[here, :]
            ds = (p.astype(F32) * (dp - delta)).astype(BF16)
            dscores[here, :] = ds
            dv = dot_t(p, g_scaled)
            dk = dot_t(ds, q_scaled)
            if piece < BLOCKS - 1:
                grad[head, 1, there, :] += dv
                grad[head, 0, there, :] += dk
            else:
                grad[head, 1, there, :] = dv
                grad[head, 0, there, :] = dk
        dq_t = dot(k_t[:, window], dscores[...]) * (inverse * SCALE)
        for index, value in enumerate((o_t, dq_t)):
            for side in range(2):
                cols = slice(side * ROWS, (side + 1) * ROWS)
                od[head, index, rows, cols] = value[:, cols].T.astype(BF16)

    send_own(0)
    pass_on(0)
    send_own(1)

    def one_head(head, carry):
        await_bytes(qd.at[head], qd_in.at[head])
        await_halo(head)
        grad[head, :, pl.ds(0, WINDOW), :] = jnp.zeros((2, WINDOW, HEAD_DIM), F32)
        transposed_keys(head)

        def one_block(block, carry):
            query_block(head, block)
            grads_first(head, block)

            @pl.when((block == 0) & (head > 0))
            def _():
                grads_second(head - 1)

            @pl.when((block == 1) & (head < HEADS - 1))
            def _():
                pass_on(head + 1)

            @pl.when((block == 1) & (head < HEADS - 2))
            def _():
                send_own(head + 2)

            @pl.when((block == 2) & (head > 1))
            def _():
                grads_last(head - 2)

            return carry

        lax.fori_loop(0, PEERS, one_block, 0)
        send_back(od.at[head, 0], 2, o_out, 0, head)
        send_back(od.at[head, 1], 2, dq_out, 1, head)
        return carry

    lax.fori_loop(0, HEADS, one_head, 0)
    grads_second(HEADS - 1)
    grads_last(HEADS - 2)
    grads_last(HEADS - 1)

    for array, buffer in enumerate((kv, kv, qd, qd)):
        region = pl.ds(0, OWN)
        await_bytes(buffer.at[pl.ds(0, PEERS - 1), 0, region, :], in_send.at[array])
    for hop in range(2):
        for head in range(HEADS):

            @pl.when(has_next)
            def _():
                halo(head, hop).wait_send()

            @pl.when(has_prev)
            def _():
                stage, buffer = ((first_stage, got_first), (second_stage, got_second))[hop]
                grad_copy(stage, buffer, hop, head).wait_send()

    for array, (out, stage) in enumerate(
        (
            (o_out, od.at[pl.ds(0, PEERS - 1), 0]),
            (dq_out, od.at[pl.ds(0, PEERS - 1), 1]),
            (dk_out, last_stage.at[pl.ds(0, PEERS - 1), 0]),
            (dv_out, last_stage.at[pl.ds(0, PEERS - 1), 1]),
        )
    ):
        await_bytes(stage, out_send.at[array])
        await_bytes(out, out_recv.at[array])


def solution(mesh):
    n_seq = mesh.shape["seq"]

    def step(queries, key_rows, value_rows, grad_out):
        def call(*refs):
            kernel(n_seq, *refs)

        flops = 5 * 2 * 256 * KEYS * HEAD_DIM * HEADS * PEERS
        return pl.pallas_call(
            call,
            name="window_attention",
            out_shape=(
                jax.ShapeDtypeStruct(queries.shape, BF16),
                jax.ShapeDtypeStruct(queries.shape, BF16),
                jax.ShapeDtypeStruct(key_rows.shape, BF16),
                jax.ShapeDtypeStruct(key_rows.shape, BF16),
            ),
            in_specs=[pl.BlockSpec(memory_space=pl.ANY)] * 4,
            out_specs=[pl.BlockSpec(memory_space=pl.ANY)] * 4,
            scratch_shapes=[
                pltpu.VMEM((HEADS, 2, SPAN, HEAD_DIM), BF16),
                pltpu.VMEM((HEADS, 2, OWN, 2 * HEAD_DIM), BF16),
                pltpu.VMEM((HEADS, 2, OWN, 2 * HEAD_DIM), BF16),
                pltpu.VMEM((HEADS, 2, SPAN, HEAD_DIM), F32),
                pltpu.VMEM((HEADS, 2, OWN, HEAD_DIM), BF16),
                pltpu.VMEM((HEADS, 2, OWN, HEAD_DIM), BF16),
                pltpu.VMEM((HEADS, 2, OWN, HEAD_DIM), BF16),
                pltpu.VMEM((HEADS, 2, OWN, HEAD_DIM), BF16),
                pltpu.VMEM((HEADS, 2, OWN, HEAD_DIM), BF16),
                pltpu.VMEM((HEAD_DIM, SPAN), BF16),
                pltpu.VMEM((HEAD_DIM, SPAN), BF16),
                pltpu.VMEM((KEYS, 2 * ROWS), F32),
                pltpu.VMEM((KEYS, 2 * ROWS), BF16),
                pltpu.VMEM((KEYS, 2 * ROWS), BF16),
                pltpu.SemaphoreType.DMA((HEADS,)),
                pltpu.SemaphoreType.DMA((HEADS,)),
                pltpu.SemaphoreType.DMA((4,)),
                pltpu.SemaphoreType.DMA((2, HEADS)),
                pltpu.SemaphoreType.DMA((2, HEADS)),
                pltpu.SemaphoreType.DMA((2, HEADS)),
                pltpu.SemaphoreType.DMA((2, HEADS)),
                pltpu.SemaphoreType.DMA((4,)),
                pltpu.SemaphoreType.DMA((4,)),
            ],
            compiler_params=pltpu.CompilerParams(
                collective_id=0, has_side_effects=True, vmem_limit_bytes=60 * 1024 * 1024
            ),
            cost_estimate=pl.CostEstimate(
                flops=flops, bytes_accessed=12 * 1024 * 1024, transcendentals=0
            ),
        )(queries, key_rows, value_rows, grad_out)

    spec = P(("seq", "kvh"), None)
    return jax.shard_map(
        step, mesh=mesh, in_specs=(spec,) * 4, out_specs=(spec,) * 4, check_vma=False
    )
```
